32 devices in a mesh: gx: 8 (over z, core), gy: 4 (over y, x).
Axes of the slice: x: 2, y: 2, z: 4, core: 2. Of those that a mesh axis runs over, the one named last changes fastest.
Arguments:
- source: float32 [128, 128, 512], P('gx', 'gy'), may hold values from -80 to 80
- conductivity: float32 [128, 128, 512], P('gx', 'gy'), may hold values from 1 to 4
Outputs:
- mid_field: float32 [128, 128, 512], P('gx', 'gy')
- new_field: float32 [128, 128, 512], P('gx', 'gy')
The draws below stay inside these ranges and needn't reach their ends.
All inputs are finite; a program needn't handle non-finite values.
Results may differ from the reference program's by a relative error of at most 0.0003.
Values sent between devices are 32-bit elements; how exact they have to be, the bound alone decides.
A program may use at most 128 MiB of HBM per device.

```python
import math
import jax
import jax.numpy as jnp
from jax import lax

NZ = 512
NX = 128
NY = 128


def draw_source(key, part):
    return jnp.clip(16.0 * jax.random.normal(key, (NX, NY, NZ), jnp.float32), -80.0, 80.0)


def levels(stream_key, extent, split, smallest, top_value):
    factor_of = 1.0
    for position, parts in split:
        steps = jax.random.uniform(jax.random.fold_in(jax.random.fold_in(stream_key, 6), position), (parts,), jnp.float32, smallest / len(split), top_value / len(split))
        factor_of = factor_of * jnp.repeat(jnp.exp(steps), extent[position] // parts).reshape((-1,) + (1,) * (len(extent) - 1 - position))
    return factor_of


def setup_inputs(seed: int = 0) -> dict:
    key_of = jax.random.split(jax.random.key(seed), 3)
    source = draw_source(jax.random.fold_in(key_of[2], 71), 0)
    conductivity = jnp.clip(jnp.exp(math.log(4.0) - 1.3862944 * jax.random.uniform(key_of[1], (NX, NY, NZ), jnp.float32) ** levels(key_of[1], (NX, NY, NZ), ((0, 8), (1, 4)), -0.2, 0.2)), 1.0, 4.0)
    return dict(source=source, conductivity=conductivity)


RATE = 4096.0


def thomas(lower, diag, upper, rhs):
    def forward(carry, row):
        cp_prev, dp_prev = carry
        low, mid, upp, right = row
        denom = mid - low * cp_prev
        cp_now = upp / denom
        dp_now = (right - low * dp_prev) / denom
        return (cp_now, dp_now), (cp_now, dp_now)

    start = (jnp.zeros_like(diag[0]), jnp.zeros_like(rhs[0]))
    _, (cps, dps) = lax.scan(forward, start, (lower, diag, upper, rhs))

    def backward(x_next, row):
        cp_now, dp_now = row
        value = dp_now - cp_now * x_next
        return value, value

    _, values = lax.scan(backward, jnp.zeros_like(rhs[0]), (cps, dps), reverse=True)
    return values


def implicit_lines(field, kappa):
    padded = jnp.pad(kappa, [(1, 1)] + [(0, 0)] * (kappa.ndim - 1))
    left = 0.5 * (padded[:-2] + padded[1:-1])
    right = 0.5 * (padded[1:-1] + padded[2:])
    return thomas(-RATE * left, 1.0 + RATE * (left + right), -RATE * right, field)


def along_first(field, kappa):
    first, second, depth = field.shape
    blocks = depth // 32
    field_blocks = field.reshape(first, second, blocks, 32).transpose(2, 0, 1, 3)
    kappa_blocks = kappa.reshape(first, second, blocks, 32).transpose(2, 0, 1, 3)
    solved = lax.map(lambda pair: implicit_lines(pair[0], pair[1]), (field_blocks, kappa_blocks))
    return solved.transpose(1, 2, 0, 3).reshape(first, second, depth)


def reference(source, conductivity):
    mid_field = along_first(source, conductivity)
    new_field = along_first(mid_field.transpose(1, 0, 2), conductivity.transpose(1, 0, 2)).transpose(1, 0, 2)
    return mid_field, new_field
```

```python
import functools

import jax
import jax.numpy as jnp
from jax import lax
from jax.experimental import pallas as pl
from jax.experimental.pallas import tpu as pltpu
from jax.sharding import PartitionSpec as P

RATE = 4096.0
HALF = 0.5 * RATE
LANE = 128
MESH = pl.DeviceIdType.MESH


def peers(axis, me, count):
    return [{axis: lax.rem(me + step, count)} for step in range(1, count)]


def resolve(get, put, count):
    ratios = []
    values = []
    ratio = None
    value = None
    for k in range(count):
        diag = get(k, 0)
        rhs = get(k, 3)
        if k + 1 < count:
            diag = diag - get(k + 1, 1)
            rhs = rhs + get(k + 1, 4)
        if k > 0:
            link = get(k, 2)
            diag = diag - link * ratio
            rhs = rhs + link * value
        inv = 1.0 / diag
        value = rhs * inv
        values.append(value)
        if k + 1 < count:
            ratio = get(k + 1, 2) * inv
            ratios.append(ratio)
    for k in range(count - 2, -1, -1):
        values[k] = values[k] + ratios[k] * values[k + 1]
    for k in range(count):
        put(k, 1, values[k])
        put(k, 0, values[k - 1] if k > 0 else jnp.zeros_like(values[0]))


def kernel(
    dims,
    src_hbm,
    kap_hbm,
    mid_hbm,
    new_hbm,
    f,
    kap,
    kap_t,
    ft,
    rx,
    tx,
    ry,
    iy,
    ty,
    mid,
    new,
    halo_x,
    halo_y,
    sx,
    gx,
    bx,
    ox,
    sy,
    gy,
    by,
    oy,
    in_sem,
    out_sem,
    halo_send,
    halo_recv,
    x_send,
    x_recv,
    xb_send,
    xb_recv,
    y_send,
    y_recv,
    yb_send,
    yb_recv,
):
    nx, ny, rows, cols, tiles, per, chunks, share_x, share_y = dims
    ix = lax.axis_index("gx")
    iy_dev = lax.axis_index("gy")
    groups_x = cols // share_x
    groups_y = rows // share_y

    def lanes(l):
        return pl.ds(pl.multiple_of(l * LANE, LANE), LANE)

    kap_in = [
        pltpu.make_async_copy(kap_hbm.at[:, lanes(l)], kap.at[l], in_sem.at[0, l])
        for l in range(tiles)
    ]
    src_in = [
        pltpu.make_async_copy(src_hbm.at[:, lanes(l)], f.at[l], in_sem.at[1, l])
        for l in range(tiles)
    ]
    for copy in kap_in + src_in:
        copy.start()

    barrier = pltpu.get_barrier_semaphore()
    for target in peers("gx", ix, nx) + peers("gy", iy_dev, ny):
        pl.semaphore_signal(barrier, inc=1, device_id=target, device_id_type=MESH)
    pl.semaphore_wait(barrier, nx + ny - 2)

    def halo(slot, source, dest, target):
        return pltpu.make_async_remote_copy(
            src_ref=source,
            dst_ref=dest,
            send_sem=halo_send.at[slot],
            recv_sem=halo_recv.at[slot],
            device_id=target,
            device_id_type=MESH,
        )

    x_up = halo(0, kap_hbm.at[pl.ds((rows - 1) * cols, cols), :], halo_x.at[0], {"gx": lax.rem(ix + 1, nx)})
    x_down = halo(1, kap_hbm.at[pl.ds(0, cols), :], halo_x.at[1], {"gx": lax.rem(ix + nx - 1, nx)})
    y_up = halo(2, kap_t.at[:, pl.ds((cols - 1) * rows, rows), :], halo_y.at[0], {"gy": lax.rem(iy_dev + 1, ny)})
    y_down = halo(3, kap_t.at[:, pl.ds(0, rows), :], halo_y.at[1], {"gy": lax.rem(iy_dev + ny - 1, ny)})

    x_up.start()
    x_down.start()

    for l in range(tiles):
        kap_in[l].wait()

    def turn(l, carry):
        for i in range(rows):
            kap_t[l, pl.ds(i, cols, stride=rows), :] = kap[l, pl.ds(i * cols, cols), :]
        return carry

    lax.fori_loop(0, tiles, turn, 0)
    y_up.start()
    y_down.start()
    x_up.wait_recv()
    x_down.wait_recv()

    @pl.when(ix == 0)
    def _():
        halo_x[0] = jnp.zeros(halo_x.shape[1:], jnp.float32)

    @pl.when(ix == nx - 1)
    def _():
        halo_x[1] = jnp.zeros(halo_x.shape[1:], jnp.float32)

    def x_forward(l, chunk, part):
        def row(i):
            return kap[l, pl.ds(i * cols, cols), :]

        here = row(0)
        face = HALF * (halo_x[0, :, lanes(l)] + here)
        total = 1.0 + face
        link = face
        y = f[l, pl.ds(0, cols), :]
        p = None
        q = None
        for i in range(rows):
            at = pl.ds(i * cols, cols)
            if i > 0:
                total = 1.0 + ratio * total
                link = ratio * link
                y = f[l, at, :] + ratio * y
            after = row(i + 1) if i + 1 < rows else halo_x[1, :, lanes(l)]
            face = HALF * (here + after)
            here = after
            diag = total + face
            if i + 1 < rows:
                inv = 1.0 / diag
                ratio = face * inv
                t = link * inv
                p = t * link if p is None else p + t * link
                q = t * y if q is None else q + t * y
                rx[l, at, :] = ratio
                tx[l, at, :] = t
                f[l, at, :] = y * inv
        slots = pl.ds(part * groups_x, groups_x)
        for coef, value in enumerate((diag, p, link, y, q)):
            sx[chunk, slots, coef] = value.reshape(groups_x, share_x, LANE)

    def exchange(axis, me, count, chunk, source, dest, send_sem, recv_sem):
        return [
            pltpu.make_async_remote_copy(
                src_ref=source.at[chunk, lax.rem(me + step, count)],
                dst_ref=dest.at[chunk, me],
                send_sem=send_sem.at[chunk, step],
                recv_sem=recv_sem.at[chunk, step],
                device_id={axis: lax.rem(me + step, count)},
                device_id_type=MESH,
            )
            for step in range(1, count)
        ]

    def arrived(axis, me, count, chunk, source, dest, send_sem, recv_sem):
        for step in range(1, count):
            origin = lax.rem(me + count - step, count)
            pltpu.make_async_remote_copy(
                src_ref=source.at[chunk, origin],
                dst_ref=dest.at[chunk, origin],
                send_sem=send_sem.at[chunk, step],
                recv_sem=recv_sem.at[chunk, step],
                device_id={axis: origin},
                device_id_type=MESH,
            ).wait_recv()

    x_up_args = lambda c: ("gx", ix, nx, c, sx, gx, x_send, x_recv)
    x_back_args = lambda c: ("gx", ix, nx, c, bx, ox, xb_send, xb_recv)
    y_up_args = lambda c: ("gy", iy_dev, ny, c, sy, gy, y_send, y_recv)
    y_back_args = lambda c: ("gy", iy_dev, ny, c, by, oy, yb_send, yb_recv)
    pending = []

    def launch(args):
        copies = exchange(*args)
        for copy in copies:
            copy.start()
        pending.extend(copies)

    for c in range(chunks):
        for a in range(per):
            src_in[c * per + a].wait()

        def body(a, carry, c=c):
            x_forward(c * per + a, c, a)
            return carry

        lax.fori_loop(0, per, body, 0)
        launch(x_up_args(c))
        gx[c, ix] = sx[c, ix]

    y_up.wait_recv()
    y_down.wait_recv()

    @pl.when(iy_dev == 0)
    def _():
        halo_y[0] = jnp.zeros(halo_y.shape[1:], jnp.float32)

    @pl.when(iy_dev == ny - 1)
    def _():
        halo_y[1] = jnp.zeros(halo_y.shape[1:], jnp.float32)

    def y_factor(c):
        part = pl.ds(c * per, per)

        def row(j):
            return kap_t[part, pl.ds(j * rows, rows), :]

        here = row(0)
        face = HALF * (halo_y[0, part] + here)
        total = 1.0 + face
        link = face
        p = None
        for j in range(cols):
            at = pl.ds(j * rows, rows)
            if j > 0:
                total = 1.0 + ratio * total
                link = ratio * link
            after = row(j + 1) if j + 1 < cols else halo_y[1, part]
            face = HALF * (here + after)
            here = after
            diag = total + face
            if j + 1 < cols:
                inv = 1.0 / diag
                ratio = face * inv
                t = link * inv
                p = t * link if p is None else p + t * link
                ry[part, at, :] = ratio
                ty[part, at, :] = t
                iy[part, at, :] = inv
        for coef, value in enumerate((diag, p, link)):
            sy[c, :, coef] = value.reshape(per * groups_y, share_y, LANE)

    def factor_body(c, carry):
        y_factor(c)
        return carry

    lax.fori_loop(0, chunks, factor_body, 0)

    def solve_ends(chunk, got, back, count):
        def get(k, coef):
            return got[chunk, k, coef]

        def put(k, which, value):
            back[chunk, k, which] = value

        resolve(get, put, count)

    for c in range(chunks):
        arrived(*x_up_args(c))
        solve_ends(c, gx, bx, nx)
        launch(x_back_args(c))
        ox[c, ix] = bx[c, ix]

    def x_backward(l, chunk, part):
        slots = pl.ds(part * groups_x, groups_x)
        before = ox[chunk, slots, 0].reshape(cols, LANE)
        m = ox[chunk, slots, 1].reshape(cols, LANE)
        for i in range(rows - 1, -1, -1):
            at = pl.ds(i * cols, cols)
            if i + 1 < rows:
                m = f[l, at, :] + tx[l, at, :] * before + rx[l, at, :] * m
            mid[l, at, :] = m
            ft[l, pl.ds(i, cols, stride=rows), :] = m

    def y_forward(c):
        part = pl.ds(c * per, per)
        q = None
        for j in range(cols):
            at = pl.ds(j * rows, rows)
            y_now = ft[part, at, :]
            if j > 0:
                y_now = y_now + ry[part, pl.ds((j - 1) * rows, rows), :] * y
            y = y_now
            if j + 1 < cols:
                step = ty[part, at, :] * y
                q = step if q is None else q + step
                ft[part, at, :] = y * iy[part, at, :]
        for coef, value in ((3, y), (4, q)):
            sy[c, :, coef] = value.reshape(per * groups_y, share_y, LANE)

    outs = []
    for c in range(chunks):
        arrived(*x_back_args(c))

        def body(a, carry, c=c):
            x_backward(c * per + a, c, a)
            return carry

        lax.fori_loop(0, per, body, 0)
        y_forward(c)
        launch(y_up_args(c))
        gy[c, iy_dev] = sy[c, iy_dev]
        for a in range(per):
            l = c * per + a
            out = pltpu.make_async_copy(mid.at[l], mid_hbm.at[:, lanes(l)], out_sem.at[0, l])
            out.start()
            outs.append(out)

    for c in range(chunks):
        arrived(*y_up_args(c))
        solve_ends(c, gy, by, ny)
        launch(y_back_args(c))
        oy[c, iy_dev] = by[c, iy_dev]

    def y_backward(c):
        part = pl.ds(c * per, per)
        before = oy[c, :, 0].reshape(per, rows, LANE)
        n = oy[c, :, 1].reshape(per, rows, LANE)
        for j in range(cols - 1, -1, -1):
            at = pl.ds(j * rows, rows)
            if j + 1 < cols:
                n = ft[part, at, :] + ty[part, at, :] * before + ry[part, at, :] * n
            for a in range(per):
                new[c * per + a, pl.ds(j, rows, stride=cols), :] = n[a]

    for c in range(chunks):
        arrived(*y_back_args(c))
        y_backward(c)
        for a in range(per):
            l = c * per + a
            out = pltpu.make_async_copy(new.at[l], new_hbm.at[:, lanes(l)], out_sem.at[1, l])
            out.start()
            outs.append(out)

    for out in outs:
        out.wait()
    for copy in [x_up, x_down, y_up, y_down] + pending:
        copy.wait_send()


def per_device(source, conductivity):
    rows, cols, depth = source.shape
    nx = lax.axis_size("gx")
    ny = lax.axis_size("gy")
    tiles = depth // LANE
    per = min(tiles, max(1, 8 * nx // cols, 8 * ny // rows if ny * 8 <= rows * tiles else 1))
    chunks = tiles // per
    share_x = cols * per // nx
    share_y = rows * per // ny
    dims = (nx, ny, rows, cols, tiles, per, chunks, share_x, share_y)
    size = rows * cols
    f32 = jnp.float32
    block = pltpu.VMEM((tiles, size, LANE), f32)
    dma = pltpu.SemaphoreType.DMA
    flat = jax.ShapeDtypeStruct((size, depth), f32)
    mid, new = pl.pallas_call(
        functools.partial(kernel, dims),
        out_shape=(flat, flat),
        in_specs=[pl.BlockSpec(memory_space=pl.ANY)] * 2,
        out_specs=(pl.BlockSpec(memory_space=pl.ANY),) * 2,
        scratch_shapes=[block] * 11
        + [
            pltpu.VMEM((2, cols, depth), f32),
            pltpu.VMEM((2, tiles, rows, LANE), f32),
            pltpu.VMEM((chunks, nx, 5, share_x, LANE), f32),
            pltpu.VMEM((chunks, nx, 5, share_x, LANE), f32),
            pltpu.VMEM((chunks, nx, 2, share_x, LANE), f32),
            pltpu.VMEM((chunks, nx, 2, share_x, LANE), f32),
            pltpu.VMEM((chunks, ny, 5, share_y, LANE), f32),
            pltpu.VMEM((chunks, ny, 5, share_y, LANE), f32),
            pltpu.VMEM((chunks, ny, 2, share_y, LANE), f32),
            pltpu.VMEM((chunks, ny, 2, share_y, LANE), f32),
            dma((2, tiles)),
            dma((2, tiles)),
            dma((4,)),
            dma((4,)),
            dma((chunks, nx)),
            dma((chunks, nx)),
            dma((chunks, nx)),
            dma((chunks, nx)),
            dma((chunks, ny)),
            dma((chunks, ny)),
            dma((chunks, ny)),
            dma((chunks, ny)),
        ],
        compiler_params=pltpu.CompilerParams(
            collective_id=0, has_side_effects=True, vmem_limit_bytes=48 << 20
        ),
    )(source.reshape(size, depth), conductivity.reshape(size, depth))
    return mid.reshape(source.shape), new.reshape(source.shape)


def solution(mesh):
    return jax.shard_map(
        per_device,
        mesh=mesh,
        in_specs=(P("gx", "gy", None), P("gx", "gy", None)),
        out_specs=(P("gx", "gy", None), P("gx", "gy", None)),
        check_vma=False,
    )
```

```python
import functools

import jax
import jax.numpy as jnp
from jax import lax
from jax.experimental import pallas as pl
from jax.experimental.pallas import tpu as pltpu
from jax.sharding import PartitionSpec as P

RATE = 4096.0
HALF = 0.5 * RATE
LANE = 128
MESH = pl.DeviceIdType.MESH


def peers(axis, me, count):
    return [{axis: lax.rem(me + step, count)} for step in range(1, count)]


def resolve(get, put, count):
    ratios = []
    values = []
    ratio = None
    value = None
    for k in range(count):
        diag = get(k, 0)
        rhs = get(k, 3)
        if k + 1 < count:
            diag = diag - get(k + 1, 1)
            rhs = rhs + get(k + 1, 4)
        if k > 0:
            link = get(k, 2)
            diag = diag - link * ratio
            rhs = rhs + link * value
        inv = 1.0 / diag
        value = rhs * inv
        values.append(value)
        if k + 1 < count:
            ratio = get(k + 1, 2) * inv
            ratios.append(ratio)
    for k in range(count - 2, -1, -1):
        values[k] = values[k] + ratios[k] * values[k + 1]
    for k in range(count):
        put(k, 1, values[k])
        put(k, 0, values[k - 1] if k > 0 else jnp.zeros_like(values[0]))


def kernel(
    dims,
    src_hbm,
    kap_hbm,
    mid,
    ft,
    ry,
    ty,
    ends,
    f,
    kap,
    kap_t,
    rx,
    tx,
    iy,
    halo_x,
    halo_y,
    sx,
    gx,
    bx,
    ox,
    sa,
    ga,
    sy,
    gy,
    by,
    oy,
    in_sem,
    halo_send,
    halo_recv,
    x_send,
    x_recv,
    xb_send,
    xb_recv,
    a_send,
    a_recv,
    y_send,
    y_recv,
    yb_send,
    yb_recv,
):
    nx, ny, rows, cols, tiles, per, chunks, share_x, share_y = dims
    ix = lax.axis_index("gx")
    iy_dev = lax.axis_index("gy")
    groups_x = cols // share_x
    groups_y = rows // share_y

    def lanes(l):
        return pl.ds(pl.multiple_of(l * LANE, LANE), LANE)

    kap_in = [
        pltpu.make_async_copy(kap_hbm.at[:, lanes(l)], kap.at[l], in_sem.at[0, l])
        for l in range(tiles)
    ]
    src_in = [
        pltpu.make_async_copy(src_hbm.at[:, lanes(l)], f.at[l], in_sem.at[1, l])
        for l in range(tiles)
    ]
    for copy in kap_in + src_in:
        copy.start()

    barrier = pltpu.get_barrier_semaphore()
    for target in peers("gx", ix, nx) + peers("gy", iy_dev, ny):
        pl.semaphore_signal(barrier, inc=1, device_id=target, device_id_type=MESH)
    pl.semaphore_wait(barrier, nx + ny - 2)

    def halo(slot, source, dest, target):
        return pltpu.make_async_remote_copy(
            src_ref=source,
            dst_ref=dest,
            send_sem=halo_send.at[slot],
            recv_sem=halo_recv.at[slot],
            device_id=target,
            device_id_type=MESH,
        )

    x_up = halo(0, kap_hbm.at[pl.ds((rows - 1) * cols, cols), :], halo_x.at[0], {"gx": lax.rem(ix + 1, nx)})
    x_down = halo(1, kap_hbm.at[pl.ds(0, cols), :], halo_x.at[1], {"gx": lax.rem(ix + nx - 1, nx)})
    y_up = halo(2, kap_t.at[:, pl.ds((cols - 1) * rows, rows), :], halo_y.at[0], {"gy": lax.rem(iy_dev + 1, ny)})
    y_down = halo(3, kap_t.at[:, pl.ds(0, rows), :], halo_y.at[1], {"gy": lax.rem(iy_dev + ny - 1, ny)})

    x_more, x_less = ix < nx - 1, ix > 0
    y_more, y_less = iy_dev < ny - 1, iy_dev > 0
    pl.when(x_more)(x_up.start)
    pl.when(x_less)(x_down.start)

    for l in range(tiles):
        kap_in[l].wait()

    def turn(l, carry):
        for i in range(rows):
            kap_t[l, pl.ds(i, cols, stride=rows), :] = kap[l, pl.ds(i * cols, cols), :]
        return carry

    lax.fori_loop(0, tiles, turn, 0)
    pl.when(y_more)(y_up.start)
    pl.when(y_less)(y_down.start)
    pl.when(x_less)(x_up.wait_recv)
    pl.when(x_more)(x_down.wait_recv)

    @pl.when(ix == 0)
    def _():
        halo_x[0] = jnp.zeros(halo_x.shape[1:], jnp.float32)

    @pl.when(ix == nx - 1)
    def _():
        halo_x[1] = jnp.zeros(halo_x.shape[1:], jnp.float32)

    def x_forward(l, chunk, part):
        def row(i):
            return kap[l, pl.ds(i * cols, cols), :]

        here = row(0)
        face = HALF * (halo_x[0, :, lanes(l)] + here)
        total = 1.0 + face
        link = face
        y = f[l, pl.ds(0, cols), :]
        p = None
        q = None
        for i in range(rows):
            at = pl.ds(i * cols, cols)
            if i > 0:
                total = 1.0 + ratio * total
                link = ratio * link
                y = f[l, at, :] + ratio * y
            after = row(i + 1) if i + 1 < rows else halo_x[1, :, lanes(l)]
            face = HALF * (here + after)
            here = after
            diag = total + face
            if i + 1 < rows:
                inv = 1.0 / diag
                ratio = face * inv
                t = link * inv
                p = t * link if p is None else p + t * link
                q = t * y if q is None else q + t * y
                rx[l, at, :] = ratio
                tx[l, at, :] = t
                f[l, at, :] = y * inv
        slots = pl.ds(part * groups_x, groups_x)
        for coef, value in enumerate((diag, p, link, y, q)):
            sx[chunk, slots, coef] = value.reshape(groups_x, share_x, LANE)

    def exchange(axis, me, count, chunk, source, dest, send_sem, recv_sem):
        return [
            pltpu.make_async_remote_copy(
                src_ref=source.at[chunk, lax.rem(me + step, count)],
                dst_ref=dest.at[chunk, me],
                send_sem=send_sem.at[chunk, step],
                recv_sem=recv_sem.at[chunk, step],
                device_id={axis: lax.rem(me + step, count)},
                device_id_type=MESH,
            )
            for step in range(1, count)
        ]

    def arrived(axis, me, count, chunk, source, dest, send_sem, recv_sem):
        for step in range(1, count):
            origin = lax.rem(me + count - step, count)
            pltpu.make_async_remote_copy(
                src_ref=source.at[chunk, origin],
                dst_ref=dest.at[chunk, origin],
                send_sem=send_sem.at[chunk, step],
                recv_sem=recv_sem.at[chunk, step],
                device_id={axis: origin},
                device_id_type=MESH,
            ).wait_recv()

    x_up_args = lambda c: ("gx", ix, nx, c, sx, gx, x_send, x_recv)
    x_back_args = lambda c: ("gx", ix, nx, c, bx, ox, xb_send, xb_recv)
    y_up_args = lambda c: ("gy", iy_dev, ny, c, sy, gy, y_send, y_recv)
    a_args = ("gy", iy_dev, ny, 0, sa, ga, a_send, a_recv)
    y_back_args = lambda c: ("gy", iy_dev, ny, c, by, oy, yb_send, yb_recv)
    pending = []

    def launch(args):
        copies = exchange(*args)
        for copy in copies:
            copy.start()
        pending.extend(copies)

    for c in range(chunks):
        for a in range(per):
            src_in[c * per + a].wait()

        def body(a, carry, c=c):
            x_forward(c * per + a, c, a)
            return carry

        lax.fori_loop(0, per, body, 0)
        launch(x_up_args(c))
        gx[c, ix] = sx[c, ix]

    pl.when(y_less)(y_up.wait_recv)
    pl.when(y_more)(y_down.wait_recv)

    @pl.when(iy_dev == 0)
    def _():
        halo_y[0] = jnp.zeros(halo_y.shape[1:], jnp.float32)

    @pl.when(iy_dev == ny - 1)
    def _():
        halo_y[1] = jnp.zeros(halo_y.shape[1:], jnp.float32)

    def y_factor(c):
        part = pl.ds(c * per, per)

        def row(j):
            return kap_t[part, pl.ds(j * rows, rows), :]

        here = row(0)
        face = HALF * (halo_y[0, part] + here)
        total = 1.0 + face
        link = face
        p = None
        for j in range(cols):
            at = pl.ds(j * rows, rows)
            if j > 0:
                total = 1.0 + ratio * total
                link = ratio * link
            after = row(j + 1) if j + 1 < cols else halo_y[1, part]
            face = HALF * (here + after)
            here = after
            diag = total + face
            if j + 1 < cols:
                inv = 1.0 / diag
                ratio = face * inv
                t = link * inv
                p = t * link if p is None else p + t * link
                ry[part, at, :] = ratio
                ty[part, at, :] = t
                iy[part, at, :] = inv
        for coef, value in enumerate((diag, p, link)):
            sa[0, :, c, coef] = value.reshape(per * groups_y, share_y, LANE)

    def factor_body(c, carry):
        y_factor(c)
        return carry

    lax.fori_loop(0, chunks, factor_body, 0)
    launch(a_args)
    ga[0, iy_dev] = sa[0, iy_dev]

    def solve_x(c):
        def get(k, coef):
            return gx[c, k, coef]

        def put(k, which, value):
            bx[c, k, which] = value

        resolve(get, put, nx)

    def solve_y(c):
        def get(k, coef):
            return ga[0, k, c, coef] if coef < 3 else gy[c, k, coef - 3]

        def put(k, which, value):
            by[c, k, which] = value

        resolve(get, put, ny)

    for c in range(chunks):
        arrived(*x_up_args(c))
        solve_x(c)
        launch(x_back_args(c))
        ox[c, ix] = bx[c, ix]

    def x_backward(l, chunk, part):
        slots = pl.ds(part * groups_x, groups_x)
        before = ox[chunk, slots, 0].reshape(cols, LANE)
        m = ox[chunk, slots, 1].reshape(cols, LANE)
        for i in range(rows - 1, -1, -1):
            at = pl.ds(i * cols, cols)
            if i + 1 < rows:
                m = f[l, at, :] + tx[l, at, :] * before + rx[l, at, :] * m
            mid[l, at, :] = m
            ft[l, pl.ds(i, cols, stride=rows), :] = m

    def y_forward(c):
        part = pl.ds(c * per, per)
        q = None
        for j in range(cols):
            at = pl.ds(j * rows, rows)
            y_now = ft[part, at, :]
            if j > 0:
                y_now = y_now + ry[part, pl.ds((j - 1) * rows, rows), :] * y
            y = y_now
            if j + 1 < cols:
                step = ty[part, at, :] * y
                q = step if q is None else q + step
                ft[part, at, :] = y * iy[part, at, :]
        for coef, value in enumerate((y, q)):
            sy[c, :, coef] = value.reshape(per * groups_y, share_y, LANE)

    for c in range(chunks):
        arrived(*x_back_args(c))

        def body(a, carry, c=c):
            x_backward(c * per + a, c, a)
            return carry

        lax.fori_loop(0, per, body, 0)
        y_forward(c)
        launch(y_up_args(c))
        gy[c, iy_dev] = sy[c, iy_dev]

    arrived(*a_args)
    for c in range(chunks):
        arrived(*y_up_args(c))
        solve_y(c)
        launch(y_back_args(c))
        oy[c, iy_dev] = by[c, iy_dev]

    for c in range(chunks):
        arrived(*y_back_args(c))
        ends[c] = oy[c]

    for copy in pending:
        copy.wait_send()
    pl.when(x_more)(x_up.wait_send)
    pl.when(x_less)(x_down.wait_send)
    pl.when(y_more)(y_up.wait_send)
    pl.when(y_less)(y_down.wait_send)


def finish(dims, mid, ft, ry, ty, ends, mid_hbm, new_hbm, new, out_sem):
    nx, ny, rows, cols, tiles, per, chunks, share_x, share_y = dims
    outs = []

    def send(source, dest, which, l):
        out = pltpu.make_async_copy(
            source.at[l], dest.at[:, pl.ds(l * LANE, LANE)], out_sem.at[which, l]
        )
        out.start()
        outs.append(out)

    for l in range(tiles):
        send(mid, mid_hbm, 0, l)
    for c in range(chunks):
        part = pl.ds(c * per, per)
        before = ends[c, :, 0].reshape(per, rows, LANE)
        n = ends[c, :, 1].reshape(per, rows, LANE)
        for j in range(cols - 1, -1, -1):
            at = pl.ds(j * rows, rows)
            if j + 1 < cols:
                n = ft[part, at, :] + ty[part, at, :] * before + ry[part, at, :] * n
            for a in range(per):
                new[c * per + a, pl.ds(j, rows, stride=cols), :] = n[a]
        for a in range(per):
            send(new, new_hbm, 1, c * per + a)
    for out in outs:
        out.wait()


def per_device(source, conductivity):
    rows, cols, depth = source.shape
    nx = lax.axis_size("gx")
    ny = lax.axis_size("gy")
    tiles = depth // LANE
    per = min(tiles, max(1, 8 * nx // cols, 8 * ny // rows if ny * 8 <= rows * tiles else 1))
    chunks = tiles // per
    share_x = cols * per // nx
    share_y = rows * per // ny
    dims = (nx, ny, rows, cols, tiles, per, chunks, share_x, share_y)
    size = rows * cols
    f32 = jnp.float32
    block = pltpu.VMEM((tiles, size, LANE), f32)
    ends = pltpu.VMEM((chunks, ny, 2, share_y, LANE), f32)
    dma = pltpu.SemaphoreType.DMA
    flat = jax.ShapeDtypeStruct((size, depth), f32)
    hbm = pl.BlockSpec(memory_space=pltpu.HBM)
    vmem = pl.BlockSpec(memory_space=pltpu.VMEM)
    parts = pl.pallas_call(
        functools.partial(kernel, dims),
        out_shape=(block,) * 4 + (ends,),
        in_specs=[hbm] * 2,
        out_specs=(vmem,) * 5,
        scratch_shapes=[block] * 6
        + [
            pltpu.VMEM((2, cols, depth), f32),
            pltpu.VMEM((2, tiles, rows, LANE), f32),
            pltpu.VMEM((chunks, nx, 5, share_x, LANE), f32),
            pltpu.VMEM((chunks, nx, 5, share_x, LANE), f32),
            pltpu.VMEM((chunks, nx, 2, share_x, LANE), f32),
            pltpu.VMEM((chunks, nx, 2, share_x, LANE), f32),
            pltpu.VMEM((1, ny, chunks, 3, share_y, LANE), f32),
            pltpu.VMEM((1, ny, chunks, 3, share_y, LANE), f32),
            pltpu.VMEM((chunks, ny, 2, share_y, LANE), f32),
            pltpu.VMEM((chunks, ny, 2, share_y, LANE), f32),
            ends,
            ends,
            dma((2, tiles)),
            dma((4,)),
            dma((4,)),
            dma((chunks, nx)),
            dma((chunks, nx)),
            dma((chunks, nx)),
            dma((chunks, nx)),
            dma((1, ny)),
            dma((1, ny)),
            dma((chunks, ny)),
            dma((chunks, ny)),
            dma((chunks, ny)),
            dma((chunks, ny)),
        ],
        compiler_params=pltpu.CompilerParams(
            collective_id=0, has_side_effects=True, vmem_limit_bytes=32 << 20
        ),
    )(*(pltpu.with_memory_space_constraint(x.reshape(size, depth), pltpu.HBM) for x in (source, conductivity)))
    mid, new = pl.pallas_call(
        functools.partial(finish, dims),
        out_shape=(flat, flat),
        in_specs=[vmem] * 5,
        out_specs=(hbm, hbm),
        scratch_shapes=[block, dma((2, tiles))],
        compiler_params=pltpu.CompilerParams(vmem_limit_bytes=32 << 20),
    )(*parts)
    return mid.reshape(source.shape), new.reshape(source.shape)


def solution(mesh):
    return jax.shard_map(
        per_device,
        mesh=mesh,
        in_specs=(P("gx", "gy", None), P("gx", "gy", None)),
        out_specs=(P("gx", "gy", None), P("gx", "gy", None)),
        check_vma=False,
    )
```

```python
import functools

import jax
import jax.numpy as jnp
from jax import lax
from jax.experimental import pallas as pl
from jax.experimental.pallas import tpu as pltpu
from jax.sharding import PartitionSpec as P

RATE = 4096.0
HALF = 0.5 * RATE
LANE = 128
MESH = pl.DeviceIdType.MESH


def peers(axis, me, count):
    return [{axis: lax.rem(me + step, count)} for step in range(1, count)]


def resolve(get, put, count):
    ratios = []
    values = []
    ratio = None
    value = None
    for k in range(count):
        diag = get(k, 0)
        rhs = get(k, 3)
        if k + 1 < count:
            diag = diag - get(k + 1, 1)
            rhs = rhs + get(k + 1, 4)
        if k > 0:
            link = get(k, 2)
            diag = diag - link * ratio
            rhs = rhs + link * value
        inv = 1.0 / diag
        value = rhs * inv
        values.append(value)
        if k + 1 < count:
            ratio = get(k + 1, 2) * inv
            ratios.append(ratio)
    for k in range(count - 2, -1, -1):
        values[k] = values[k] + ratios[k] * values[k + 1]
    for k in range(count):
        put(k, 1, values[k])
        put(k, 0, values[k - 1] if k > 0 else jnp.zeros_like(values[0]))


def kernel(
    dims,
    src_hbm,
    kap_hbm,
    mid,
    ft,
    ry,
    ty,
    ends,
    f,
    kap,
    kap_t,
    rx,
    tx,
    iy,
    halo_x,
    halo_y,
    sx,
    ab,
    zx,
    gz,
    bz,
    oz,
    tri,
    ox,
    sa,
    ga,
    sy,
    gy,
    by,
    oy,
    in_sem,
    halo_send,
    halo_recv,
    pair_send,
    pair_recv,
    z_send,
    z_recv,
    zb_send,
    zb_recv,
    pb_send,
    pb_recv,
    a_send,
    a_recv,
    y_send,
    y_recv,
    yb_send,
    yb_recv,
):
    nx, ny, rows, cols, tiles, per, chunks, share_x, share_y = dims
    ix = lax.axis_index("gx")
    iy_dev = lax.axis_index("gy")
    nz = nx // 2
    core = lax.rem(ix, 2)
    iz = lax.div(ix, 2)
    partner = {"gx": ix + 1 - 2 * core}
    groups_x = cols // share_x
    groups_y = rows // share_y

    def lanes(l):
        return pl.ds(pl.multiple_of(l * LANE, LANE), LANE)

    kap_in = [
        pltpu.make_async_copy(kap_hbm.at[:, lanes(l)], kap.at[l], in_sem.at[0, l])
        for l in range(tiles)
    ]
    src_in = [
        pltpu.make_async_copy(src_hbm.at[:, lanes(l)], f.at[l], in_sem.at[1, l])
        for l in range(tiles)
    ]
    for copy in kap_in + src_in:
        copy.start()

    barrier = pltpu.get_barrier_semaphore()
    for target in peers("gx", ix, nx) + peers("gy", iy_dev, ny):
        pl.semaphore_signal(barrier, inc=1, device_id=target, device_id_type=MESH)
    pl.semaphore_wait(barrier, nx + ny - 2)

    def halo(slot, source, dest, target):
        return pltpu.make_async_remote_copy(
            src_ref=source,
            dst_ref=dest,
            send_sem=halo_send.at[slot],
            recv_sem=halo_recv.at[slot],
            device_id=target,
            device_id_type=MESH,
        )

    x_up = halo(0, kap_hbm.at[pl.ds((rows - 1) * cols, cols), :], halo_x.at[0], {"gx": lax.rem(ix + 1, nx)})
    x_down = halo(1, kap_hbm.at[pl.ds(0, cols), :], halo_x.at[1], {"gx": lax.rem(ix + nx - 1, nx)})
    y_up = halo(2, kap_t.at[:, pl.ds((cols - 1) * rows, rows), :], halo_y.at[0], {"gy": lax.rem(iy_dev + 1, ny)})
    y_down = halo(3, kap_t.at[:, pl.ds(0, rows), :], halo_y.at[1], {"gy": lax.rem(iy_dev + ny - 1, ny)})

    x_more, x_less = ix < nx - 1, ix > 0
    y_more, y_less = iy_dev < ny - 1, iy_dev > 0
    pl.when(x_more)(x_up.start)
    pl.when(x_less)(x_down.start)

    for l in range(tiles):
        kap_in[l].wait()

    def turn(l, carry):
        for i in range(rows):
            kap_t[l, pl.ds(i, cols, stride=rows), :] = kap[l, pl.ds(i * cols, cols), :]
        return carry

    lax.fori_loop(0, tiles, turn, 0)
    pl.when(y_more)(y_up.start)
    pl.when(y_less)(y_down.start)
    pl.when(x_less)(x_up.wait_recv)
    pl.when(x_more)(x_down.wait_recv)

    @pl.when(ix == 0)
    def _():
        halo_x[0] = jnp.zeros(halo_x.shape[1:], jnp.float32)

    @pl.when(ix == nx - 1)
    def _():
        halo_x[1] = jnp.zeros(halo_x.shape[1:], jnp.float32)

    def x_forward(l, chunk, part):
        def row(i):
            return kap[l, pl.ds(i * cols, cols), :]

        here = row(0)
        face = HALF * (halo_x[0, :, lanes(l)] + here)
        total = 1.0 + face
        link = face
        y = f[l, pl.ds(0, cols), :]
        p = None
        q = None
        for i in range(rows):
            at = pl.ds(i * cols, cols)
            if i > 0:
                total = 1.0 + ratio * total
                link = ratio * link
                y = f[l, at, :] + ratio * y
            after = row(i + 1) if i + 1 < rows else halo_x[1, :, lanes(l)]
            face = HALF * (here + after)
            here = after
            diag = total + face
            if i + 1 < rows:
                inv = 1.0 / diag
                ratio = face * inv
                t = link * inv
                p = t * link if p is None else p + t * link
                q = t * y if q is None else q + t * y
                rx[l, at, :] = ratio
                tx[l, at, :] = t
                f[l, at, :] = y * inv
        slots = pl.ds(part * groups_x, groups_x)
        for coef, value in enumerate((diag, p, link, y, q)):
            sx[chunk, slots, coef] = value.reshape(groups_x, share_x, LANE)

    def place(axis, index):
        return {"gx": 2 * index + core} if axis == "z" else {axis: index}

    def exchange(axis, me, count, chunk, source, dest, send_sem, recv_sem):
        return [
            pltpu.make_async_remote_copy(
                src_ref=source.at[chunk, lax.rem(me + step, count)],
                dst_ref=dest.at[chunk, me],
                send_sem=send_sem.at[chunk, step],
                recv_sem=recv_sem.at[chunk, step],
                device_id=place(axis, lax.rem(me + step, count)),
                device_id_type=MESH,
            )
            for step in range(1, count)
        ]

    def arrived(axis, me, count, chunk, source, dest, send_sem, recv_sem):
        for step in range(1, count):
            origin = lax.rem(me + count - step, count)
            pltpu.make_async_remote_copy(
                src_ref=source.at[chunk, origin],
                dst_ref=dest.at[chunk, origin],
                send_sem=send_sem.at[chunk, step],
                recv_sem=recv_sem.at[chunk, step],
                device_id=place(axis, origin),
                device_id_type=MESH,
            ).wait_recv()

    x_up_args = lambda c: ("z", iz, nz, c, zx, gz, z_send, z_recv)
    x_back_args = lambda c: ("z", iz, nz, c, bz, oz, zb_send, zb_recv)
    own_half = pl.ds(core * nz, nz)
    other_half = pl.ds((1 - core) * nz, nz)

    def pair_up(c):
        return pltpu.make_async_remote_copy(
            src_ref=sx.at[c, other_half],
            dst_ref=ab.at[c, core],
            send_sem=pair_send.at[c],
            recv_sem=pair_recv.at[c],
            device_id=partner,
            device_id_type=MESH,
        )

    def pair_back(c):
        return pltpu.make_async_remote_copy(
            src_ref=tri.at[c, pl.ds(1 - core, 2)],
            dst_ref=ox.at[c, :, own_half],
            send_sem=pb_send.at[c],
            recv_sem=pb_recv.at[c],
            device_id=partner,
            device_id_type=MESH,
        )

    def merge(c):
        diag = ab[c, 0, :, 0] - ab[c, 1, :, 1]
        inv = 1.0 / diag
        low = ab[c, 0, :, 2]
        high = ab[c, 1, :, 2]
        base = (ab[c, 0, :, 3] + ab[c, 1, :, 4]) * inv
        to_low = low * inv
        to_high = high * inv
        zx[c, :, 0] = ab[c, 1, :, 0] - high * to_high
        zx[c, :, 1] = ab[c, 0, :, 1] + low * to_low
        zx[c, :, 2] = low * to_high
        zx[c, :, 3] = ab[c, 1, :, 3] + high * base
        zx[c, :, 4] = ab[c, 0, :, 4] + low * base
        return base, to_low, to_high
    y_up_args = lambda c: ("gy", iy_dev, ny, c, sy, gy, y_send, y_recv)
    a_args = ("gy", iy_dev, ny, 0, sa, ga, a_send, a_recv)
    y_back_args = lambda c: ("gy", iy_dev, ny, c, by, oy, yb_send, yb_recv)
    pending = []

    def launch(args):
        copies = exchange(*args)
        for copy in copies:
            copy.start()
        pending.extend(copies)

    for c in range(chunks):
        for a in range(per):
            src_in[c * per + a].wait()

        def body(a, carry, c=c):
            x_forward(c * per + a, c, a)
            return carry

        lax.fori_loop(0, per, body, 0)
        copy = pair_up(c)
        copy.start()
        pending.append(copy)
        ab[c, core] = sx[c, own_half]

    merged = []
    for c in range(chunks):
        pair_up(c).wait_recv()
        merged.append(merge(c))
        launch(x_up_args(c))
        gz[c, iz] = zx[c, iz]

    pl.when(y_less)(y_up.wait_recv)
    pl.when(y_more)(y_down.wait_recv)

    @pl.when(iy_dev == 0)
    def _():
        halo_y[0] = jnp.zeros(halo_y.shape[1:], jnp.float32)

    @pl.when(iy_dev == ny - 1)
    def _():
        halo_y[1] = jnp.zeros(halo_y.shape[1:], jnp.float32)

    def y_factor(c):
        part = pl.ds(c * per, per)

        def row(j):
            return kap_t[part, pl.ds(j * rows, rows), :]

        here = row(0)
        face = HALF * (halo_y[0, part] + here)
        total = 1.0 + face
        link = face
        p = None
        for j in range(cols):
            at = pl.ds(j * rows, rows)
            if j > 0:
                total = 1.0 + ratio * total
                link = ratio * link
            after = row(j + 1) if j + 1 < cols else halo_y[1, part]
            face = HALF * (here + after)
            here = after
            diag = total + face
            if j + 1 < cols:
                inv = 1.0 / diag
                ratio = face * inv
                t = link * inv
                p = t * link if p is None else p + t * link
                ry[part, at, :] = ratio
                ty[part, at, :] = t
                iy[part, at, :] = inv
        for coef, value in enumerate((diag, p, link)):
            sa[0, :, c, coef] = value.reshape(per * groups_y, share_y, LANE)

    def factor_body(c, carry):
        y_factor(c)
        return carry

    lax.fori_loop(0, chunks, factor_body, 0)
    launch(a_args)
    ga[0, iy_dev] = sa[0, iy_dev]

    def solve_x(c):
        def get(k, coef):
            return gz[c, k, coef]

        def put(k, which, value):
            bz[c, k, which] = value

        resolve(get, put, nz)

    def solve_y(c):
        def get(k, coef):
            return ga[0, k, c, coef] if coef < 3 else gy[c, k, coef - 3]

        def put(k, which, value):
            by[c, k, which] = value

        resolve(get, put, ny)

    for c in range(chunks):
        arrived(*x_up_args(c))
        solve_x(c)
        launch(x_back_args(c))
        oz[c, iz] = bz[c, iz]

    def x_backward(l, chunk, part):
        slots = pl.ds(part * groups_x, groups_x)
        before = ox[chunk, 0, slots].reshape(cols, LANE)
        m = ox[chunk, 1, slots].reshape(cols, LANE)
        for i in range(rows - 1, -1, -1):
            at = pl.ds(i * cols, cols)
            if i + 1 < rows:
                m = f[l, at, :] + tx[l, at, :] * before + rx[l, at, :] * m
            mid[l, at, :] = m
            ft[l, pl.ds(i, cols, stride=rows), :] = m

    def y_forward(c):
        part = pl.ds(c * per, per)
        q = None
        for j in range(cols):
            at = pl.ds(j * rows, rows)
            y_now = ft[part, at, :]
            if j > 0:
                y_now = y_now + ry[part, pl.ds((j - 1) * rows, rows), :] * y
            y = y_now
            if j + 1 < cols:
                step = ty[part, at, :] * y
                q = step if q is None else q + step
                ft[part, at, :] = y * iy[part, at, :]
        for coef, value in enumerate((y, q)):
            sy[c, :, coef] = value.reshape(per * groups_y, share_y, LANE)

    for c in range(chunks):
        arrived(*x_back_args(c))
        base, to_low, to_high = merged[c]
        before = oz[c, :, 0]
        last = oz[c, :, 1]
        tri[c, 0] = before
        tri[c, 1] = base + to_low * before + to_high * last
        tri[c, 2] = last
        copy = pair_back(c)
        copy.start()
        pending.append(copy)
        ox[c, :, own_half] = tri[c, pl.ds(core, 2)]

    for c in range(chunks):
        pair_back(c).wait_recv()

        def body(a, carry, c=c):
            x_backward(c * per + a, c, a)
            return carry

        lax.fori_loop(0, per, body, 0)
        y_forward(c)
        launch(y_up_args(c))
        gy[c, iy_dev] = sy[c, iy_dev]

    arrived(*a_args)
    for c in range(chunks):
        arrived(*y_up_args(c))
        solve_y(c)
        launch(y_back_args(c))
        oy[c, iy_dev] = by[c, iy_dev]

    for c in range(chunks):
        arrived(*y_back_args(c))
        ends[c] = oy[c]

    for copy in pending:
        copy.wait_send()
    pl.when(x_more)(x_up.wait_send)
    pl.when(x_less)(x_down.wait_send)
    pl.when(y_more)(y_up.wait_send)
    pl.when(y_less)(y_down.wait_send)


def finish(dims, mid, ft, ry, ty, ends, mid_hbm, new_hbm, new, out_sem):
    nx, ny, rows, cols, tiles, per, chunks, share_x, share_y = dims
    outs = []

    def send(source, dest, which, l):
        out = pltpu.make_async_copy(
            source.at[l], dest.at[:, pl.ds(l * LANE, LANE)], out_sem.at[which, l]
        )
        out.start()
        outs.append(out)

    for l in range(tiles):
        send(mid, mid_hbm, 0, l)
    for c in range(chunks):
        part = pl.ds(c * per, per)
        before = ends[c, :, 0].reshape(per, rows, LANE)
        n = ends[c, :, 1].reshape(per, rows, LANE)
        for j in range(cols - 1, -1, -1):
            at = pl.ds(j * rows, rows)
            if j + 1 < cols:
                n = ft[part, at, :] + ty[part, at, :] * before + ry[part, at, :] * n
            for a in range(per):
                new[c * per + a, pl.ds(j, rows, stride=cols), :] = n[a]
        for a in range(per):
            send(new, new_hbm, 1, c * per + a)
    for out in outs:
        out.wait()


def per_device(source, conductivity):
    rows, cols, depth = source.shape
    nx = lax.axis_size("gx")
    ny = lax.axis_size("gy")
    tiles = depth // LANE
    per = min(tiles, max(1, 8 * nx // cols, 8 * ny // rows if ny * 8 <= rows * tiles else 1))
    chunks = tiles // per
    share_x = cols * per // nx
    share_y = rows * per // ny
    dims = (nx, ny, rows, cols, tiles, per, chunks, share_x, share_y)
    size = rows * cols
    nz = nx // 2
    f32 = jnp.float32
    block = pltpu.VMEM((tiles, size, LANE), f32)
    ends = pltpu.VMEM((chunks, ny, 2, share_y, LANE), f32)
    dma = pltpu.SemaphoreType.DMA
    flat = jax.ShapeDtypeStruct((size, depth), f32)
    hbm = pl.BlockSpec(memory_space=pltpu.HBM)
    vmem = pl.BlockSpec(memory_space=pltpu.VMEM)
    parts = pl.pallas_call(
        functools.partial(kernel, dims),
        out_shape=(block,) * 4 + (ends,),
        in_specs=[hbm] * 2,
        out_specs=(vmem,) * 5,
        scratch_shapes=[block] * 6
        + [
            pltpu.VMEM((2, cols, depth), f32),
            pltpu.VMEM((2, tiles, rows, LANE), f32),
            pltpu.VMEM((chunks, nx, 5, share_x, LANE), f32),
            pltpu.VMEM((chunks, 2, nz, 5, share_x, LANE), f32),
            pltpu.VMEM((chunks, nz, 5, share_x, LANE), f32),
            pltpu.VMEM((chunks, nz, 5, share_x, LANE), f32),
            pltpu.VMEM((chunks, nz, 2, share_x, LANE), f32),
            pltpu.VMEM((chunks, nz, 2, share_x, LANE), f32),
            pltpu.VMEM((chunks, 3, nz, share_x, LANE), f32),
            pltpu.VMEM((chunks, 2, nx, share_x, LANE), f32),
            pltpu.VMEM((1, ny, chunks, 3, share_y, LANE), f32),
            pltpu.VMEM((1, ny, chunks, 3, share_y, LANE), f32),
            pltpu.VMEM((chunks, ny, 2, share_y, LANE), f32),
            pltpu.VMEM((chunks, ny, 2, share_y, LANE), f32),
            ends,
            ends,
            dma((2, tiles)),
            dma((4,)),
            dma((4,)),
            dma((chunks,)),
            dma((chunks,)),
            dma((chunks, nz)),
            dma((chunks, nz)),
            dma((chunks, nz)),
            dma((chunks, nz)),
            dma((chunks,)),
            dma((chunks,)),
            dma((1, ny)),
            dma((1, ny)),
            dma((chunks, ny)),
            dma((chunks, ny)),
            dma((chunks, ny)),
            dma((chunks, ny)),
        ],
        compiler_params=pltpu.CompilerParams(
            collective_id=0, has_side_effects=True, vmem_limit_bytes=32 << 20
        ),
    )(*(pltpu.with_memory_space_constraint(x.reshape(size, depth), pltpu.HBM) for x in (source, conductivity)))
    mid, new = pl.pallas_call(
        functools.partial(finish, dims),
        out_shape=(flat, flat),
        in_specs=[vmem] * 5,
        out_specs=(hbm, hbm),
        scratch_shapes=[block, dma((2, tiles))],
        compiler_params=pltpu.CompilerParams(vmem_limit_bytes=32 << 20),
    )(*parts)
    return mid.reshape(source.shape), new.reshape(source.shape)


def solution(mesh):
    return jax.shard_map(
        per_device,
        mesh=mesh,
        in_specs=(P("gx", "gy", None), P("gx", "gy", None)),
        out_specs=(P("gx", "gy", None), P("gx", "gy", None)),
        check_vma=False,
    )
```

```python
import functools

import jax
import jax.numpy as jnp
from jax import lax
from jax.experimental import pallas as pl
from jax.experimental.pallas import tpu as pltpu
from jax.sharding import PartitionSpec as P

RATE = 4096.0
HALF = 0.5 * RATE
LANE = 128
MESH = pl.DeviceIdType.MESH


def peers(axis, me, count):
    return [{axis: lax.rem(me + step, count)} for step in range(1, count)]


def resolve(get, put, count):
    ratios = []
    values = []
    ratio = None
    value = None
    for k in range(count):
        diag = get(k, 0)
        rhs = get(k, 3)
        if k + 1 < count:
            diag = diag - get(k + 1, 1)
            rhs = rhs + get(k + 1, 4)
        if k > 0:
            link = get(k, 2)
            diag = diag - link * ratio
            rhs = rhs + link * value
        inv = 1.0 / diag
        value = rhs * inv
        values.append(value)
        if k + 1 < count:
            ratio = get(k + 1, 2) * inv
            ratios.append(ratio)
    for k in range(count - 2, -1, -1):
        values[k] = values[k] + ratios[k] * values[k + 1]
    for k in range(count):
        put(k, 1, values[k])
        put(k, 0, values[k - 1] if k > 0 else jnp.zeros_like(values[0]))


def kernel(
    dims,
    src_hbm,
    kap_hbm,
    mid,
    ft,
    ry,
    ty,
    ends,
    f,
    kap,
    kap_t,
    rx,
    tx,
    iy,
    halo_x,
    halo_y,
    sx,
    ab,
    zx,
    gz,
    bz,
    oz,
    tri,
    ox,
    sa,
    ga,
    sy,
    gy,
    by,
    oy,
    in_sem,
    halo_send,
    halo_recv,
    pair_send,
    pair_recv,
    z_send,
    z_recv,
    zb_send,
    zb_recv,
    pb_send,
    pb_recv,
    a_send,
    a_recv,
    y_send,
    y_recv,
    yb_send,
    yb_recv,
):
    nx, ny, rows, cols, tiles, per, chunks, share_x, share_y = dims
    ix = lax.axis_index("gx")
    iy_dev = lax.axis_index("gy")
    nz = nx // 2
    core = lax.rem(ix, 2)
    iz = lax.div(ix, 2)
    partner = {"gx": ix + 1 - 2 * core}
    groups_x = cols // share_x
    groups_y = rows // share_y

    def lanes(l):
        return pl.ds(pl.multiple_of(l * LANE, LANE), LANE)

    kap_in = [
        pltpu.make_async_copy(kap_hbm.at[:, lanes(l)], kap.at[l], in_sem.at[0, l])
        for l in range(tiles)
    ]
    src_in = [
        pltpu.make_async_copy(src_hbm.at[:, lanes(l)], f.at[l], in_sem.at[1, l])
        for l in range(tiles)
    ]
    for copy in kap_in + src_in:
        copy.start()

    barrier = pltpu.get_barrier_semaphore()
    for target in peers("gx", ix, nx) + peers("gy", iy_dev, ny):
        pl.semaphore_signal(barrier, inc=1, device_id=target, device_id_type=MESH)
    pl.semaphore_wait(barrier, nx + ny - 2)

    def halo(slot, source, dest, target):
        return pltpu.make_async_remote_copy(
            src_ref=source,
            dst_ref=dest,
            send_sem=halo_send.at[slot],
            recv_sem=halo_recv.at[slot],
            device_id=target,
            device_id_type=MESH,
        )

    x_edge = halo(0, kap_hbm.at[pl.ds((1 - core) * ((rows - 1) * cols), cols), :], halo_x, partner)
    y_up = halo(2, kap_t.at[:, pl.ds((cols - 1) * rows, rows), :], halo_y.at[0], {"gy": lax.rem(iy_dev + 1, ny)})
    y_down = halo(3, kap_t.at[:, pl.ds(0, rows), :], halo_y.at[1], {"gy": lax.rem(iy_dev + ny - 1, ny)})

    y_more, y_less = iy_dev < ny - 1, iy_dev > 0
    x_edge.start()

    for l in range(tiles):
        kap_in[l].wait()

    def turn(l, carry):
        for i in range(rows):
            kap_t[l, pl.ds(i, cols, stride=rows), :] = kap[l, pl.ds(i * cols, cols), :]
        return carry

    lax.fori_loop(0, tiles, turn, 0)
    pl.when(y_more)(y_up.start)
    pl.when(y_less)(y_down.start)
    x_edge.wait_recv()
    lower = core == 0

    def x_forward(l, chunk, part):
        def row(i):
            return kap[l, pl.ds(i * cols, cols), :]

        here = row(0)
        first = here
        source = f[l, pl.ds(0, cols), :]
        face = HALF * (halo_x[:, lanes(l)] + here)
        total = 1.0 + face
        link = face
        y = source
        for i in range(rows):
            at = pl.ds(i * cols, cols)
            if i == 1:
                total = 1.0 + jnp.where(lower, face, ratio * total)
                link = jnp.where(lower, face, ratio * link)
                y = f[l, at, :] + jnp.where(lower, 0.0, ratio * y)
            elif i > 1:
                total = 1.0 + ratio * total
                link = ratio * link
                y = f[l, at, :] + ratio * y
            after = row(i + 1) if i + 1 < rows else halo_x[:, lanes(l)]
            face = HALF * (here + after)
            if i + 1 == rows:
                face = jnp.where(lower, face, 0.0)
                edge = jnp.where(lower, first, here)
            here = after
            diag = total + face
            if i == 0:
                inv = 1.0 / diag
                ratio = face * inv
                t = link * inv
                p = jnp.where(lower, -1.0 - face, t * link)
                q = jnp.where(lower, source, t * y)
                rx[l, at, :] = jnp.where(lower, 0.0, ratio)
                tx[l, at, :] = jnp.where(lower, 1.0, t)
                f[l, at, :] = jnp.where(lower, 0.0, y * inv)
            elif i + 1 < rows:
                inv = 1.0 / diag
                ratio = face * inv
                t = link * inv
                p = p + t * link
                q = q + t * y
                rx[l, at, :] = ratio
                tx[l, at, :] = t
                f[l, at, :] = y * inv
        slots = pl.ds(part * groups_x, groups_x)
        for coef, value in enumerate((diag, p, link, y, q, edge)):
            sx[chunk, slots, coef] = value.reshape(groups_x, share_x, LANE)

    def place(axis, index):
        return {"gx": 2 * index + core} if axis == "z" else {axis: index}

    def exchange(axis, me, count, chunk, source, dest, send_sem, recv_sem):
        return [
            pltpu.make_async_remote_copy(
                src_ref=source.at[chunk, lax.rem(me + step, count)],
                dst_ref=dest.at[chunk, me],
                send_sem=send_sem.at[chunk, step],
                recv_sem=recv_sem.at[chunk, step],
                device_id=place(axis, lax.rem(me + step, count)),
                device_id_type=MESH,
            )
            for step in range(1, count)
        ]

    def arrived(axis, me, count, chunk, source, dest, send_sem, recv_sem):
        for step in range(1, count):
            origin = lax.rem(me + count - step, count)
            pltpu.make_async_remote_copy(
                src_ref=source.at[chunk, origin],
                dst_ref=dest.at[chunk, origin],
                send_sem=send_sem.at[chunk, step],
                recv_sem=recv_sem.at[chunk, step],
                device_id=place(axis, origin),
                device_id_type=MESH,
            ).wait_recv()

    x_up_args = lambda c: ("z", iz, nz, c, zx, gz, z_send, z_recv)
    x_back_args = lambda c: ("z", iz, nz, c, bz, oz, zb_send, zb_recv)
    own_half = pl.ds(core * nz, nz)
    other_half = pl.ds((1 - core) * nz, nz)

    def pair_up(c):
        return pltpu.make_async_remote_copy(
            src_ref=sx.at[c, other_half],
            dst_ref=ab.at[c, core],
            send_sem=pair_send.at[c],
            recv_sem=pair_recv.at[c],
            device_id=partner,
            device_id_type=MESH,
        )

    def pair_back(c):
        return pltpu.make_async_remote_copy(
            src_ref=tri.at[c, pl.ds(1 - core, 2)],
            dst_ref=ox.at[c, :, own_half],
            send_sem=pb_send.at[c],
            recv_sem=pb_recv.at[c],
            device_id=partner,
            device_id_type=MESH,
        )

    def merge(c):
        diag = ab[c, 0, :, 0] - ab[c, 1, :, 1]
        inv = 1.0 / diag
        low = ab[c, 0, :, 2]
        high = ab[c, 1, :, 2]
        base = (ab[c, 0, :, 3] + ab[c, 1, :, 4]) * inv
        to_low = low * inv
        to_high = high * inv
        zx[c, :, 0] = ab[c, 1, :, 0] - high * to_high
        zx[c, :, 1] = ab[c, 0, :, 1] + low * to_low
        zx[c, :, 2] = low * to_high
        zx[c, :, 3] = ab[c, 1, :, 3] + high * base
        zx[c, :, 4] = ab[c, 0, :, 4] + low * base
        zx[c, :, 5] = ab[c, 0, :, 5]
        zx[c, :, 6] = ab[c, 1, :, 5]
        return base, to_low, to_high
    y_up_args = lambda c: ("gy", iy_dev, ny, c, sy, gy, y_send, y_recv)
    a_args = ("gy", iy_dev, ny, 0, sa, ga, a_send, a_recv)
    y_back_args = lambda c: ("gy", iy_dev, ny, c, by, oy, yb_send, yb_recv)
    pending = []

    def launch(args):
        copies = exchange(*args)
        for copy in copies:
            copy.start()
        pending.extend(copies)

    for c in range(chunks):
        for a in range(per):
            src_in[c * per + a].wait()

        def body(a, carry, c=c):
            x_forward(c * per + a, c, a)
            return carry

        lax.fori_loop(0, per, body, 0)
        copy = pair_up(c)
        copy.start()
        pending.append(copy)
        ab[c, core] = sx[c, own_half]

    merged = []
    for c in range(chunks):
        pair_up(c).wait_recv()
        merged.append(merge(c))
        launch(x_up_args(c))
        gz[c, iz] = zx[c, iz]

    pl.when(y_less)(y_up.wait_recv)
    pl.when(y_more)(y_down.wait_recv)

    @pl.when(iy_dev == 0)
    def _():
        halo_y[0] = jnp.zeros(halo_y.shape[1:], jnp.float32)

    @pl.when(iy_dev == ny - 1)
    def _():
        halo_y[1] = jnp.zeros(halo_y.shape[1:], jnp.float32)

    def y_factor(c):
        part = pl.ds(c * per, per)

        def row(j):
            return kap_t[part, pl.ds(j * rows, rows), :]

        here = row(0)
        face = HALF * (halo_y[0, part] + here)
        total = 1.0 + face
        link = face
        p = None
        for j in range(cols):
            at = pl.ds(j * rows, rows)
            if j > 0:
                total = 1.0 + ratio * total
                link = ratio * link
            after = row(j + 1) if j + 1 < cols else halo_y[1, part]
            face = HALF * (here + after)
            here = after
            diag = total + face
            if j + 1 < cols:
                inv = 1.0 / diag
                ratio = face * inv
                t = link * inv
                p = t * link if p is None else p + t * link
                ry[part, at, :] = ratio
                ty[part, at, :] = t
                iy[part, at, :] = inv
        for coef, value in enumerate((diag, p, link)):
            sa[0, :, c, coef] = value.reshape(per * groups_y, share_y, LANE)

    def factor_body(c, carry):
        y_factor(c)
        return carry

    lax.fori_loop(0, chunks, factor_body, 0)
    launch(a_args)
    ga[0, iy_dev] = sa[0, iy_dev]

    def solve_x(c):
        below = [HALF * gz[c, k, 5] for k in range(nz)]
        above = [HALF * gz[c, k, 6] for k in range(nz)]
        face = [below[k] + above[k - 1] if k > 0 else below[0] for k in range(nz)] + [above[-1]]
        parts = []
        firsts = []
        for k in range(nz):
            inv = 1.0 / (face[k] - gz[c, k, 1])
            link = gz[c, k, 2]
            drive = gz[c, k, 4] * inv
            to_low = face[k] * inv
            to_high = link * inv
            firsts.append((drive, to_low, to_high))
            parts.append(
                (
                    gz[c, k, 0] + face[k + 1] - link * to_high,
                    face[k] * to_low,
                    link * to_low,
                    gz[c, k, 3] + link * drive,
                    face[k] * drive,
                )
            )
        ends = {}

        def put(k, which, value):
            ends[k, which] = value

        resolve(lambda k, coef: parts[k][coef], put, nz)
        for k in range(nz):
            drive, to_low, to_high = firsts[k]
            bz[c, k, 0] = drive + to_low * ends[k, 0] + to_high * ends[k, 1]
            bz[c, k, 1] = ends[k, 1]

    def solve_y(c):
        def get(k, coef):
            return ga[0, k, c, coef] if coef < 3 else gy[c, k, coef - 3]

        def put(k, which, value):
            by[c, k, which] = value

        resolve(get, put, ny)

    for c in range(chunks):
        arrived(*x_up_args(c))
        solve_x(c)
        launch(x_back_args(c))
        oz[c, iz] = bz[c, iz]

    def x_backward(l, chunk, part):
        slots = pl.ds(part * groups_x, groups_x)
        before = ox[chunk, 0, slots].reshape(cols, LANE)
        m = ox[chunk, 1, slots].reshape(cols, LANE)
        for i in range(rows - 1, -1, -1):
            at = pl.ds(i * cols, cols)
            if i + 1 < rows:
                m = f[l, at, :] + tx[l, at, :] * before + rx[l, at, :] * m
            mid[l, at, :] = m
            ft[l, pl.ds(i, cols, stride=rows), :] = m

    def y_forward(c):
        part = pl.ds(c * per, per)
        q = None
        for j in range(cols):
            at = pl.ds(j * rows, rows)
            y_now = ft[part, at, :]
            if j > 0:
                y_now = y_now + ry[part, pl.ds((j - 1) * rows, rows), :] * y
            y = y_now
            if j + 1 < cols:
                step = ty[part, at, :] * y
                q = step if q is None else q + step
                ft[part, at, :] = y * iy[part, at, :]
        for coef, value in enumerate((y, q)):
            sy[c, :, coef] = value.reshape(per * groups_y, share_y, LANE)

    for c in range(chunks):
        arrived(*x_back_args(c))
        base, to_low, to_high = merged[c]
        before = oz[c, :, 0]
        last = oz[c, :, 1]
        tri[c, 0] = before
        tri[c, 1] = base + to_low * before + to_high * last
        tri[c, 2] = last
        copy = pair_back(c)
        copy.start()
        pending.append(copy)
        ox[c, :, own_half] = tri[c, pl.ds(core, 2)]

    for c in range(chunks):
        pair_back(c).wait_recv()

        def body(a, carry, c=c):
            x_backward(c * per + a, c, a)
            return carry

        lax.fori_loop(0, per, body, 0)
        y_forward(c)
        launch(y_up_args(c))
        gy[c, iy_dev] = sy[c, iy_dev]

    arrived(*a_args)
    for c in range(chunks):
        arrived(*y_up_args(c))
        solve_y(c)
        launch(y_back_args(c))
        oy[c, iy_dev] = by[c, iy_dev]

    for c in range(chunks):
        arrived(*y_back_args(c))
        ends[c] = oy[c]

    for copy in pending:
        copy.wait_send()
    x_edge.wait_send()
    pl.when(y_more)(y_up.wait_send)
    pl.when(y_less)(y_down.wait_send)


def finish(dims, mid, ft, ry, ty, ends, mid_hbm, new_hbm, new, out_sem):
    nx, ny, rows, cols, tiles, per, chunks, share_x, share_y = dims
    outs = []

    def send(source, dest, which, l):
        out = pltpu.make_async_copy(
            source.at[l], dest.at[:, pl.ds(l * LANE, LANE)], out_sem.at[which, l]
        )
        out.start()
        outs.append(out)

    for l in range(tiles):
        send(mid, mid_hbm, 0, l)
    for c in range(chunks):
        part = pl.ds(c * per, per)
        before = ends[c, :, 0].reshape(per, rows, LANE)
        n = ends[c, :, 1].reshape(per, rows, LANE)
        for j in range(cols - 1, -1, -1):
            at = pl.ds(j * rows, rows)
            if j + 1 < cols:
                n = ft[part, at, :] + ty[part, at, :] * before + ry[part, at, :] * n
            for a in range(per):
                new[c * per + a, pl.ds(j, rows, stride=cols), :] = n[a]
        for a in range(per):
            send(new, new_hbm, 1, c * per + a)
    for out in outs:
        out.wait()


def per_device(source, conductivity):
    rows, cols, depth = source.shape
    nx = lax.axis_size("gx")
    ny = lax.axis_size("gy")
    tiles = depth // LANE
    per = min(tiles, max(1, 8 * nx // cols, 8 * ny // rows if ny * 8 <= rows * tiles else 1))
    chunks = tiles // per
    share_x = cols * per // nx
    share_y = rows * per // ny
    dims = (nx, ny, rows, cols, tiles, per, chunks, share_x, share_y)
    size = rows * cols
    nz = nx // 2
    f32 = jnp.float32
    block = pltpu.VMEM((tiles, size, LANE), f32)
    ends = pltpu.VMEM((chunks, ny, 2, share_y, LANE), f32)
    dma = pltpu.SemaphoreType.DMA
    flat = jax.ShapeDtypeStruct((size, depth), f32)
    hbm = pl.BlockSpec(memory_space=pltpu.HBM)
    vmem = pl.BlockSpec(memory_space=pltpu.VMEM)
    parts = pl.pallas_call(
        functools.partial(kernel, dims),
        out_shape=(block,) * 4 + (ends,),
        in_specs=[hbm] * 2,
        out_specs=(vmem,) * 5,
        scratch_shapes=[block] * 6
        + [
            pltpu.VMEM((cols, depth), f32),
            pltpu.VMEM((2, tiles, rows, LANE), f32),
            pltpu.VMEM((chunks, nx, 6, share_x, LANE), f32),
            pltpu.VMEM((chunks, 2, nz, 6, share_x, LANE), f32),
            pltpu.VMEM((chunks, nz, 7, share_x, LANE), f32),
            pltpu.VMEM((chunks, nz, 7, share_x, LANE), f32),
            pltpu.VMEM((chunks, nz, 2, share_x, LANE), f32),
            pltpu.VMEM((chunks, nz, 2, share_x, LANE), f32),
            pltpu.VMEM((chunks, 3, nz, share_x, LANE), f32),
            pltpu.VMEM((chunks, 2, nx, share_x, LANE), f32),
            pltpu.VMEM((1, ny, chunks, 3, share_y, LANE), f32),
            pltpu.VMEM((1, ny, chunks, 3, share_y, LANE), f32),
            pltpu.VMEM((chunks, ny, 2, share_y, LANE), f32),
            pltpu.VMEM((chunks, ny, 2, share_y, LANE), f32),
            ends,
            ends,
            dma((2, tiles)),
            dma((4,)),
            dma((4,)),
            dma((chunks,)),
            dma((chunks,)),
            dma((chunks, nz)),
            dma((chunks, nz)),
            dma((chunks, nz)),
            dma((chunks, nz)),
            dma((chunks,)),
            dma((chunks,)),
            dma((1, ny)),
            dma((1, ny)),
            dma((chunks, ny)),
            dma((chunks, ny)),
            dma((chunks, ny)),
            dma((chunks, ny)),
        ],
        compiler_params=pltpu.CompilerParams(
            collective_id=0, has_side_effects=True, vmem_limit_bytes=32 << 20
        ),
    )(*(pltpu.with_memory_space_constraint(x.reshape(size, depth), pltpu.HBM) for x in (source, conductivity)))
    mid, new = pl.pallas_call(
        functools.partial(finish, dims),
        out_shape=(flat, flat),
        in_specs=[vmem] * 5,
        out_specs=(hbm, hbm),
        scratch_shapes=[block, dma((2, tiles))],
        compiler_params=pltpu.CompilerParams(vmem_limit_bytes=32 << 20),
    )(*parts)
    return mid.reshape(source.shape), new.reshape(source.shape)


def solution(mesh):
    return jax.shard_map(
        per_device,
        mesh=mesh,
        in_specs=(P("gx", "gy", None), P("gx", "gy", None)),
        out_specs=(P("gx", "gy", None), P("gx", "gy", None)),
        check_vma=False,
    )
```
